128 devices in a mesh: segment: 4 (over x), col: 32 (over z, y, core).
Axes of the slice: x: 4, y: 4, z: 4, core: 2. Of those that a mesh axis runs over, the one named last changes fastest.
Arguments:
- left_env: bfloat16 [384, 8192], P(None, 'col'), may hold values from -6 to 6
- bit_strings: int32 [384, 4], P(None, 'segment'), may hold values from 0 to 1
- site_tensors: bfloat16 [4, 2, 8192, 8192], P('segment', None, None, 'col'), may hold values from -0.0625 to 0.0625
Outputs:
- section_env: bfloat16 [4, 384, 8192], P('segment', None, 'col')
- section_log: float32 [4, 384], P('segment')
The draws below stay inside these ranges and needn't reach their ends.
All inputs are finite; a program needn't handle non-finite values. Where the reference program divides by a largest or mean magnitude, that divisor is 1e-20 or more.
Results may differ from the reference program's by a relative error of at most 0.0065.
Values may be sent and summed in bfloat16 or wider, within the bound.
No kernel may reach another device: no remote copies, remote signals or barrier semaphores. Data moves between devices by JAX's collectives and lax.ppermute only.
A program may use at most 128 MiB of HBM per device.

```python
import jax
import jax.numpy as jnp
from jax import lax

CHI = 8192
PHYS = 2
ROWS = 384
SITES_SEGMENT = 1
SECTIONS = 4
SITES = 4


def touch_ends(array, key, smallest, largest):
    spot = [jax.random.randint(jax.random.fold_in(key, axis), (), 0, length) for axis, length in enumerate(array.shape)]
    main_axis = array.shape.index(max(array.shape))
    neighbour = spot[:main_axis] + [(spot[main_axis] + 1) % array.shape[main_axis]] + spot[main_axis + 1:]
    return array.at[tuple(spot)].set(smallest).at[tuple(neighbour)].set(largest)


def steps_of(stream_key, dims, cuts, low, largest):
    gain = 1.0
    for dim, blocks in cuts:
        steps = jax.random.uniform(jax.random.fold_in(jax.random.fold_in(stream_key, 6), dim), (blocks,), jnp.float32, low / len(cuts), largest / len(cuts))
        gain = gain * jnp.repeat(jnp.exp(steps), dims[dim] // blocks).reshape((-1,) + (1,) * (len(dims) - 1 - dim))
    return gain


def bell_draw(key, dims, scale, limit, shards=(), held_as=jnp.bfloat16):
    result = jax.random.normal(key, dims, jnp.float32) * scale
    if len(shards) > 0:
        result = steps_of(key, dims, shards, -0.22, 0.18) * result
    return jnp.clip(result, min=-limit, max=limit).astype(held_as)


def setup_inputs(seed: int = 0) -> dict:
    streams_of = jax.random.split(jax.random.key(seed), 4)
    left_env = bell_draw(streams_of[0], (ROWS, CHI), 1.0, 6.0, ((1, 32),))
    bit_strings = touch_ends(jax.random.randint(streams_of[1], (ROWS, SITES), 0, 2), jax.random.fold_in(streams_of[1], 1), 0, 1).astype(jnp.int32)
    site_tensors = bell_draw(streams_of[2], (SITES, PHYS, CHI, CHI), CHI ** -0.5, 0.0625, ((0, 4), (3, 32)))
    return dict(left_env=left_env, bit_strings=bit_strings, site_tensors=site_tensors)


def reference(left_env, bit_strings, site_tensors):
    vector = left_env
    env_list = []
    log_list = []
    for section in range(SECTIONS):
        log_total = jnp.zeros((ROWS,), jnp.float32)
        for inner in range(SITES_SEGMENT):
            site_index = section * SITES_SEGMENT + inner
            operand = vector.astype(jnp.float32)
            product_zero = jnp.dot(operand, site_tensors[site_index, 0].astype(jnp.float32), precision=lax.Precision.HIGHEST)
            product_one = jnp.dot(operand, site_tensors[site_index, 1].astype(jnp.float32), precision=lax.Precision.HIGHEST)
            chosen = jnp.where(bit_strings[:, site_index:site_index + 1] == 1, product_one, product_zero)
            maximum = jnp.max(jnp.abs(chosen), axis=1) + jnp.float32(1e-6)
            vector = (chosen / maximum[:, None]).astype(jnp.bfloat16)
            log_total = log_total + jnp.log(maximum)
        env_list.append(vector)
        log_list.append(log_total)
    return jnp.stack(env_list), jnp.stack(log_list)
```

```python
import functools

import jax
import jax.numpy as jnp
from jax import lax
from jax.experimental import pallas as pl
from jax.experimental.pallas import tpu as pltpu
from jax.sharding import PartitionSpec as P

MICRO = 4
EXTRA = 16

epsilon = 1e-06


def kernel(blocks, core_ref, own_ref, other_ref, bit_ref, tensor_ref, block_ref, product_ref, largest_ref):
    rows = product_ref.shape[0]
    width = product_ref.shape[1]
    core = core_ref[0]

    def add_on(i, carry):
        total_zero, total_one, largest = carry
        for ref, side in ((own_ref, core), (other_ref, 1 - core)):
            start = pl.multiple_of((2 * i + side) * width, width)
            piece = ref[i, :rows, :]
            total_zero += jnp.dot(
                piece, tensor_ref[0, pl.ds(start, width), :], preferred_element_type=jnp.float32
            )
            total_one += jnp.dot(
                piece, tensor_ref[1, pl.ds(start, width), :], preferred_element_type=jnp.float32
            )
            parts = ref[i, rows:, :].astype(jnp.float32)
            largest = jnp.maximum(largest, (parts[0:1] + parts[1:2]) + parts[2:3])
        return total_zero, total_one, largest

    zeros = jnp.zeros((rows, width), jnp.float32)
    carry = (zeros, zeros, jnp.zeros((1, width), jnp.float32))
    for i in range(blocks):
        carry = add_on(i, carry)
    total_zero, total_one, largest = carry
    divisor = jnp.broadcast_to(largest, (8, width)).T[:rows, 0:1]
    product = jnp.where(bit_ref[...] == 1, total_one, total_zero) / divisor
    product_ref[...] = product
    block_ref[:rows, :] = product.astype(jnp.bfloat16)
    local = jnp.max(jnp.abs(product), axis=1, keepdims=True) + epsilon
    local = jnp.concatenate([local, jnp.zeros((width - rows, 1), jnp.float32)], axis=0)
    local = jnp.broadcast_to(local, (width, 128)).T[0:8]
    largest_ref[...] = local
    high = local.astype(jnp.bfloat16).astype(jnp.float32)
    rest = local - high
    middle = rest.astype(jnp.bfloat16).astype(jnp.float32)
    low = rest - middle
    row = lax.broadcasted_iota(jnp.int32, (EXTRA, width), 0)
    extra = jnp.where(
        row == 0, high[0:1], jnp.where(row == 1, middle[0:1], jnp.where(row == 2, low[0:1], 0.0))
    )
    block_ref[rows:, :] = extra.astype(jnp.bfloat16)


def site(core, own, other, bits, tensor):
    blocks, height, width = own.shape
    rows = height - EXTRA
    vmem = pl.BlockSpec(memory_space=pltpu.VMEM)
    return pl.pallas_call(
        functools.partial(kernel, blocks),
        out_shape=(
            jax.ShapeDtypeStruct((height, width), jnp.bfloat16),
            jax.ShapeDtypeStruct((rows, width), jnp.float32),
            jax.ShapeDtypeStruct((8, width), jnp.float32),
        ),
        in_specs=[pl.BlockSpec(memory_space=pltpu.SMEM), vmem, vmem, vmem, vmem],
        out_specs=(vmem, vmem, vmem),
        compiler_params=pltpu.CompilerParams(vmem_limit_bytes=40 * 1024 * 1024),
        name="site",
    )(core, own, other, bits, tensor)


def local(left_env, bit_strings, site_tensors):
    segments = lax.axis_size("segment")
    segment = lax.axis_index("segment")
    cols = lax.axis_size("col")
    chips = cols // 2
    core = (lax.axis_index("col") % 2).reshape(1)
    row_count, width = left_env.shape
    rows = row_count // MICRO
    tensor = site_tensors[0]
    same_core = [[2 * i + c for i in range(chips)] for c in range(2)]
    swap = [(i, i ^ 1) for i in range(cols)]
    forward = [(i, i + 1) for i in range(segments - 1)]
    ones = jnp.where(
        lax.broadcasted_iota(jnp.int32, (EXTRA, width), 0) == 0, 1.0, 0.0
    ).astype(jnp.bfloat16)

    ticks = MICRO + segments - 1
    incoming = None
    products, maxima = [], []
    for tick in range(ticks):
        batch = min(tick, MICRO - 1)
        first = jnp.concatenate([left_env[batch * rows:(batch + 1) * rows], ones], axis=0)
        current = first if incoming is None else jnp.where(segment == 0, first, incoming)
        own = lax.all_to_all(
            jnp.broadcast_to(current[None], (chips, *current.shape)),
            "col", 0, 0, axis_index_groups=same_core, tiled=True,
        )
        other = lax.ppermute(own, "col", swap)
        position = jnp.clip(tick - segment, 0, MICRO - 1)
        bits = lax.dynamic_slice_in_dim(bit_strings, position * rows, rows, 0)
        block, product, largest = site(core, own, other, bits, tensor)
        products.append(product)
        maxima.append(largest[0, :rows])
        if tick + 1 < ticks:
            incoming = lax.ppermute(block, "segment", forward)

    largest = lax.dynamic_slice_in_dim(jnp.stack(maxima), segment, MICRO, 0)
    everything = lax.all_to_all(
        jnp.broadcast_to(largest[None], (cols, *largest.shape)), "col", 0, 0, tiled=True
    )
    maximum = jnp.max(everything, axis=0)
    product = lax.dynamic_slice_in_dim(jnp.stack(products), segment, MICRO, 0)
    env = (product / maximum[:, :, None]).astype(jnp.bfloat16)
    return env.reshape(1, row_count, width), jnp.log(maximum).reshape(1, row_count)


def solution(mesh):
    placed = (P(None, "col"), P(None, "segment"), P("segment", None, None, "col"))
    return jax.shard_map(
        local,
        mesh=mesh,
        in_specs=placed,
        out_specs=(P("segment", None, "col"), P("segment", None)),
        check_vma=False,
    )
```

```python
import functools

import jax
import jax.numpy as jnp
from jax import lax
from jax.experimental import pallas as pl
from jax.experimental.pallas import tpu as pltpu
from jax.sharding import PartitionSpec as P

KINDS = "a"
BATCHES = 3
RING = 4
STEPS = (0, 1, 3, 2)

epsilon = 1e-06


def pieces_of(kind, z, y, core, refs):
    if kind == "a":
        own_ref, other_ref = refs
        for chip in range(RING * RING):
            yield chip, ((own_ref, chip, core), (other_ref, chip, 1 - core))
        return
    for index, ref in enumerate(refs):
        holder = core ^ (index // RING)
        from_z = (z - STEPS[index % RING]) & (RING - 1)
        for step in range(2):
            from_y = (y - 2 * holder - step) & (RING - 1)
            yield from_z * RING + from_y, tuple(
                (ref, 2 * step + side, holder ^ side) for side in range(2)
            )


def site_kernel(kind, slot, batches, tick, following, place_ref, *refs):
    count = 2 if kind == "a" else 2 * RING
    held_refs = refs[:count]
    bit_ref, left_ref, tensor_ref, block_ref, product_ref, largest_ref, *streaming = refs[count:]
    near_ref, arrived = streaming or (tensor_ref, None)
    rows, width = product_ref.shape
    segment, z, y, core = (place_ref[i] for i in range(4))
    work = []
    for k, (chip, pieces) in enumerate(pieces_of(kind, z, y, core, held_refs)):
        start = chip * 2 * width
        if not isinstance(start, int):
            start = pl.multiple_of(start, 2 * width)
        if not streaming:
            work.append((start, None, pieces))
            continue
        copy = pltpu.make_async_copy(
            tensor_ref.at[:, pl.ds(start, 2 * width), :],
            near_ref.at[:, k * 2 * width:(k + 1) * 2 * width, :],
            arrived.at[k],
        )
        copy.start()
        work.append((k * 2 * width, copy, pieces))
    zero = jnp.zeros((rows, width), jnp.float32)
    one = jnp.zeros((rows, width), jnp.float32)
    largest = jnp.zeros((rows, width), jnp.bfloat16)
    for base, copy, pieces in work:
        if copy is not None:
            copy.wait()
        for ref, index, side in pieces:
            start = pl.multiple_of(base + side * width, width)
            piece = ref[index]
            zero += jnp.dot(piece, near_ref[0, pl.ds(start, width), :], preferred_element_type=jnp.float32)
            one += jnp.dot(piece, near_ref[1, pl.ds(start, width), :], preferred_element_type=jnp.float32)
            largest = jnp.maximum(largest, jnp.abs(piece))
    divisor = jnp.max(largest.astype(jnp.float32), axis=1, keepdims=True) + epsilon
    divisor = jnp.where(segment == 0, 1.0, divisor)
    position = slot + jnp.clip(tick - segment, 0, batches - 1)
    bits = bit_ref[pl.ds(pl.multiple_of(position * rows, 8), rows), :]
    product = jnp.where(bits == 1, one, zero) / divisor
    product_ref[...] = product
    local = jnp.max(jnp.abs(product), axis=1, keepdims=True) + epsilon
    local = jnp.concatenate([local, jnp.zeros((width - rows, 1), jnp.float32)], axis=0)
    largest_ref[...] = jnp.broadcast_to(local, (width, 128)).T[0:8]
    following = left_ref[following * rows:(following + 1) * rows, :]
    block_ref[...] = jnp.where(segment == RING - 1, following, product.astype(jnp.bfloat16))


def site(kind, slot, batches, tick, following, place, held, bits, left, tensor):
    rows, width = held[0].shape[1:]
    vmem = pl.BlockSpec(memory_space=pltpu.VMEM)
    streaming = len(KINDS) > 1
    return pl.pallas_call(
        functools.partial(site_kernel, kind, slot, batches, tick, following),
        out_shape=(
            jax.ShapeDtypeStruct((rows, width), jnp.bfloat16),
            jax.ShapeDtypeStruct((rows, width), jnp.float32),
            jax.ShapeDtypeStruct((8, width), jnp.float32),
        ),
        in_specs=[pl.BlockSpec(memory_space=pltpu.SMEM)]
        + [vmem] * (len(held) + 2)
        + [pl.BlockSpec(memory_space=pltpu.HBM if streaming else pltpu.VMEM)],
        out_specs=(vmem, vmem, vmem),
        scratch_shapes=[
            pltpu.VMEM(tensor.shape, tensor.dtype),
            pltpu.SemaphoreType.DMA((RING * RING,)),
        ] if streaming else [],
        compiler_params=pltpu.CompilerParams(vmem_limit_bytes=24 * 1024 * 1024),
        name="site",
    )(place, *held, bits, left, tensor)


def collect_kernel(ticks, place_ref, *refs):
    largest_refs, maxima_ref = refs[:-1], refs[-1]
    batches = ticks - RING + 1
    lanes = maxima_ref.shape[2]
    for segment in range(RING):
        @pl.when(place_ref[0] == segment)
        def _():
            taken = [
                largest_refs[stream * ticks + batch + segment][0:1, :lanes]
                for stream in range(len(largest_refs) // ticks)
                for batch in range(batches)
            ]
            taken = jnp.concatenate(taken, axis=0)
            for i in range(maxima_ref.shape[0]):
                maxima_ref[i] = taken


def collect(cols, ticks, count, place, largest):
    vmem = pl.BlockSpec(memory_space=pltpu.VMEM)
    return pl.pallas_call(
        functools.partial(collect_kernel, ticks),
        out_shape=jax.ShapeDtypeStruct((cols, count, 128), jnp.float32),
        in_specs=[pl.BlockSpec(memory_space=pltpu.SMEM)] + [vmem] * len(largest),
        out_specs=vmem,
        name="collect",
    )(place, *largest)


def finish_kernel(ticks, place_ref, maxima_ref, *refs):
    product_refs, (env_ref, log_ref) = refs[:-2], refs[-2:]
    batches = ticks - RING + 1
    rows, width = product_refs[0].shape
    maximum = jnp.max(maxima_ref[...], axis=0)
    log_ref[...] = jnp.log(maximum)
    for slot in range(maximum.shape[0]):
        column = jnp.broadcast_to(maximum[slot:slot + 1], (8, maximum.shape[1])).T[:rows, 0:1]
        stream, batch = slot // batches, slot % batches
        for segment in range(RING):
            @pl.when(place_ref[0] == segment)
            def _():
                product = product_refs[stream * ticks + batch + segment][...]
                env_ref[slot * rows:(slot + 1) * rows, :] = (product / column).astype(jnp.bfloat16)


def finish(ticks, place, maxima, products):
    rows, width = products[0].shape
    count = maxima.shape[1]
    vmem = pl.BlockSpec(memory_space=pltpu.VMEM)
    return pl.pallas_call(
        functools.partial(finish_kernel, ticks),
        out_shape=(
            jax.ShapeDtypeStruct((count * rows, width), jnp.bfloat16),
            jax.ShapeDtypeStruct((count, maxima.shape[2]), jnp.float32),
        ),
        in_specs=[pl.BlockSpec(memory_space=pltpu.SMEM)] + [vmem] * (1 + len(products)),
        out_specs=(vmem, vmem),
        compiler_params=pltpu.CompilerParams(vmem_limit_bytes=16 * 1024 * 1024),
        name="finish",
    )(place, maxima, *products)


def moved(value, where):
    places = [
        (s, z, y, c)
        for s in range(RING) for z in range(RING) for y in range(RING) for c in range(2)
    ]
    number = {place: i for i, place in enumerate(places)}
    pairs = []
    for place in places:
        s, z, y, c = where(*place)
        pairs.append((number[place], number[(s % RING, z % RING, y % RING, c)]))
    return lax.ppermute(value, ("segment", "col"), pairs)


def swapped(value):
    return moved(value, lambda s, z, y, c: (s, z, y, 1 - c))


def after(values, *others):
    return lax.optimization_barrier((tuple(values), others))[0]


def local(left_env, bit_strings, site_tensors):
    cols = lax.axis_size("col")
    col = lax.axis_index("col")
    place = jnp.stack(
        [lax.axis_index("segment"), col // (2 * RING), (col // 2) % RING, col % 2]
    ).astype(jnp.int32)
    row_count, width = left_env.shape
    streams = len(KINDS)
    rows = row_count // (streams * BATCHES)
    ticks = BATCHES + RING - 1
    tensor = site_tensors[0]
    same_core = [[2 * i + c for i in range(cols // 2)] for c in range(2)]
    products = [[] for _ in range(streams)]
    largest = [[] for _ in range(streams)]
    last = None

    def ordered(values):
        return values if last is None or streams == 1 else after(values, last)

    def hop(kind, block):
        if kind == "a":
            return block, [moved(block, lambda s, z, y, c: (s + 1, z, y, c))]
        both = jnp.stack([block, swapped(block)])
        return both, [
            moved(both, lambda s, z, y, c, d=d: (s + 1, z, y + 2 * c + d, c)) for d in range(2)
        ]

    def spread(kind, arriving):
        if kind == "a":
            many = jnp.broadcast_to(arriving[0][None], (cols // 2, *arriving[0].shape))
            return many, [
                lax.all_to_all(many, "col", 0, 0, axis_index_groups=same_core, tiled=True)
            ]
        own = jnp.concatenate(arriving)
        return own, [
            own if d == 0 else moved(own, lambda s, z, y, c, d=d: (s, z + d, y, c)) for d in STEPS
        ]

    def compute(stream, tick, held):
        held = list(held)
        held = held + [swapped(piece) for piece in held]
        following = stream * BATCHES + min(tick + 1, BATCHES - 1)
        block, product, most = site(
            KINDS[stream], stream * BATCHES, BATCHES, tick, following, place, held,
            bit_strings, left_env, tensor,
        )
        products[stream].append(product)
        largest[stream].append(most)
        return block

    held = [None] * streams
    for stream, kind in enumerate(KINDS):
        start = stream * BATCHES * rows
        block = left_env[start:start + rows]
        arriving = [block] if kind == "a" else hop(kind, block)[1]
        last, held[stream] = spread(kind, arriving)
    for tick in range(ticks):
        for stream, kind in enumerate(KINDS):
            last = compute(stream, tick, ordered(held[stream]))
            if tick + 1 < ticks:
                last, arriving = hop(kind, last)
                last, held[stream] = spread(kind, arriving)

    maxima = collect(cols, ticks, streams * BATCHES, place, sum(largest, []))
    everything = lax.all_to_all(maxima, "col", 0, 0, tiled=True)
    env, log = finish(ticks, place, everything, sum(products, []))
    return env[None], log[:, :rows].reshape(1, row_count)


def solution(mesh):
    placed = (P(None, "col"), P(None, "segment"), P("segment", None, None, "col"))
    return jax.shard_map(
        local,
        mesh=mesh,
        in_specs=placed,
        out_specs=(P("segment", None, "col"), P("segment", None)),
        check_vma=False,
    )
```

```python
import functools

import jax
import jax.numpy as jnp
from jax import lax
from jax.experimental import pallas as pl
from jax.experimental.pallas import tpu as pltpu
from jax.sharding import PartitionSpec as P

BATCHES = 3
RING = 4

epsilon = 1e-06

VMEM = pl.BlockSpec(memory_space=pltpu.VMEM)
SMEM = pl.BlockSpec(memory_space=pltpu.SMEM)
LIMIT = pltpu.CompilerParams(vmem_limit_bytes=24 * 1024 * 1024)


def chips_of(z, y, holder):
    sign = 1 - 2 * holder
    for step_y, step_z in ((0, 0), (0, sign), (1, 0), (-1, sign)):
        for step in range(2):
            from_y = (y - step_y - 2 * holder) & (RING - 1)
            from_z = (z - step_z - 2 * step) & (RING - 1)
            yield from_z * RING + from_y


def as_column(row, rows):
    lanes = row.shape[1]
    return jnp.broadcast_to(row, (8, lanes)).T[:rows, 0:1]


def as_row(column, lanes):
    rows = column.shape[0]
    if rows < lanes:
        column = jnp.concatenate([column, jnp.zeros((lanes - rows, 1), jnp.float32)], axis=0)
    return jnp.broadcast_to(column, (lanes, 128)).T[0:8]


def hold_kernel(tensor_ref, after_ref, held_ref, arrived):
    copies = []
    pieces = arrived.shape[0]
    depth = tensor_ref.shape[1] // pieces
    for k in range(pieces):
        part = pl.ds(k * depth, depth)
        copy = pltpu.make_async_copy(tensor_ref.at[:, part, :], held_ref.at[:, part, :], arrived.at[k])
        copy.start()
        copies.append(copy)
    for copy in copies:
        copy.wait()


def hold(tensor, after):
    return pl.pallas_call(
        hold_kernel,
        out_shape=jax.ShapeDtypeStruct(tensor.shape, tensor.dtype),
        in_specs=[pl.BlockSpec(memory_space=pltpu.HBM), pl.BlockSpec(memory_space=pl.ANY)],
        out_specs=VMEM,
        scratch_shapes=[pltpu.SemaphoreType.DMA((4,))],
        compiler_params=LIMIT,
        name="hold",
    )(pltpu.with_memory_space_constraint(tensor, pltpu.HBM), after)


def site_kernel(tick, following, batches, place_ref, *refs):
    held_refs, refs = refs[:2 * RING], refs[2 * RING:]
    bit_ref, tensor_ref, refs = refs[0], refs[1], refs[2:]
    rows, width = held_refs[0].shape[1:]
    segment, z, y, core = (place_ref[i] for i in range(4))
    work = []
    for group in range(2):
        holder = core ^ group
        for k, chip in enumerate(chips_of(z, y, holder)):
            for side in range(2):
                start = pl.multiple_of((chip * 2 + (holder ^ side)) * width, width)
                work.append((held_refs[group * RING + k // 2], 2 * (k % 2) + side, start))
    totals = [jnp.zeros((rows, width), jnp.float32) for _ in range(2)]
    largest = jnp.zeros((rows, width), jnp.bfloat16)
    for ref, index, start in work:
        piece = ref[index]
        for bit in range(2):
            totals[bit] += jnp.dot(
                piece, tensor_ref[bit, pl.ds(start, width), :], preferred_element_type=jnp.float32
            )
        largest = jnp.maximum(largest, jnp.abs(piece))
    divisor = jnp.max(largest.astype(jnp.float32), axis=1, keepdims=True) + epsilon
    divisor = jnp.where(segment == 0, 1.0, divisor)
    position = jnp.clip(tick - segment, 0, batches - 1)
    bits = as_column(bit_ref[pl.ds(position, 1), :].astype(jnp.float32), rows)
    product = jnp.where(bits > 0.5, totals[1], totals[0]) / divisor
    local = as_row(jnp.max(jnp.abs(product), axis=1, keepdims=True) + epsilon, width)
    if following is None:
        largest_refs, (product_ref, maxima_ref) = refs[:-2], refs[-2:]
        product_ref[...] = product
        everything = [ref[0:1, :] for ref in largest_refs] + [local[0:1]]
        lanes = maxima_ref.shape[2]
        for segment_here in range(RING):
            @pl.when(segment == segment_here)
            def _():
                taken = jnp.concatenate(everything[segment_here:segment_here + batches], axis=0)
                for i in range(maxima_ref.shape[0]):
                    maxima_ref[i] = taken[:, :lanes]
        return
    left_ref, product_ref, largest_ref, block_ref = refs
    product_ref[...] = product
    largest_ref[...] = local
    block_ref[...] = jnp.where(
        segment == RING - 1, left_ref[pl.ds(following * rows, rows), :], product.astype(jnp.bfloat16)
    )


def site(tick, following, place, held, bits, tensor, extra, cols):
    rows, width = held[0].shape[1:]
    batches = bits.shape[0]
    product = jax.ShapeDtypeStruct((rows, width), jnp.float32)
    if following is None:
        lanes = -(-rows // 128) * 128
        out_shape = (product, jax.ShapeDtypeStruct((cols, batches, lanes), jnp.float32))
    else:
        out_shape = (
            product,
            jax.ShapeDtypeStruct((8, width), jnp.float32),
            jax.ShapeDtypeStruct((rows, width), jnp.bfloat16),
        )
    return pl.pallas_call(
        functools.partial(site_kernel, tick, following, batches),
        out_shape=out_shape,
        in_specs=[SMEM] + [VMEM] * (len(held) + 2 + len(extra)),
        out_specs=(VMEM,) * len(out_shape),
        compiler_params=LIMIT,
        name="site",
    )(place, *held, bits, tensor, *extra)


def finish_kernel(place_ref, maxima_ref, *refs):
    product_refs, (env_ref, log_ref) = refs[:-2], refs[-2:]
    rows, width = product_refs[0].shape
    maximum = jnp.max(maxima_ref[...], axis=0)
    log_ref[...] = jnp.log(maximum)
    for batch in range(maximum.shape[0]):
        column = as_column(maximum[batch:batch + 1], rows)
        for segment in range(RING):
            @pl.when(place_ref[0] == segment)
            def _():
                product = product_refs[batch + segment][...]
                env_ref[0, batch * rows:(batch + 1) * rows, :] = (product / column).astype(jnp.bfloat16)


def finish(place, maxima, products):
    rows, width = products[0].shape
    batches = maxima.shape[1]
    return pl.pallas_call(
        finish_kernel,
        out_shape=(
            jax.ShapeDtypeStruct((1, batches * rows, width), jnp.bfloat16),
            jax.ShapeDtypeStruct((batches, maxima.shape[2]), jnp.float32),
        ),
        in_specs=[SMEM] + [VMEM] * (1 + len(products)),
        out_specs=(VMEM, VMEM),
        compiler_params=LIMIT,
        name="finish",
    )(place, maxima, *products)


def moved(value, where):
    places = [
        (s, z, y, c)
        for s in range(RING) for z in range(RING) for y in range(RING) for c in range(2)
    ]
    number = {place: i for i, place in enumerate(places)}
    pairs = []
    for place in places:
        s, z, y, c = where(*place)
        pairs.append((number[place], number[(s % RING, z % RING, y % RING, c)]))
    return lax.ppermute(value, ("segment", "col"), pairs)


def swapped(value):
    return moved(value, lambda s, z, y, c: (s, z, y, 1 - c))


def gathered(block):
    both = jnp.stack([block, swapped(block)])
    first = jnp.concatenate([
        moved(both, lambda s, z, y, c, d=d: (s + 1, z + 2 * d, y + 2 * c, c)) for d in range(2)
    ])
    return [
        first,
        moved(first, lambda s, z, y, c: (s, z + 1 - 2 * c, y, c)),
        moved(first, lambda s, z, y, c: (s, z, y + 1, c)),
        moved(first, lambda s, z, y, c: (s, z + 1 - 2 * c, y - 1, c)),
    ]


def local(left_env, bit_strings, site_tensors):
    cols = lax.axis_size("col")
    col = lax.axis_index("col")
    place = jnp.stack(
        [lax.axis_index("segment"), col // (2 * RING), (col // 2) % RING, col % 2]
    ).astype(jnp.int32)
    row_count, width = left_env.shape
    rows = row_count // BATCHES
    ticks = BATCHES + RING - 1
    bits = bit_strings.reshape(BATCHES, rows)
    block, tensor = left_env[:rows], None
    products, largest = [], []
    for tick in range(ticks):
        held = gathered(block)
        if tensor is None:
            tensor = hold(site_tensors[0], held[0])
            held, tensor, bits, place = lax.optimization_barrier((held, tensor, bits, place))
        held += [swapped(piece) for piece in held]
        if tick + 1 < ticks:
            following = min(tick + 1, BATCHES - 1)
            product, most, block = site(tick, following, place, held, bits, tensor, [left_env], cols)
            largest.append(most)
        else:
            product, maxima = site(tick, None, place, held, bits, tensor, largest, cols)
        products.append(product)

    maxima = lax.all_to_all(maxima, "col", 0, 0, tiled=True)
    env, log = finish(place, maxima, products)
    return env, log[:, :rows].reshape(1, row_count)


def solution(mesh):
    placed = (P(None, "col"), P(None, "segment"), P("segment", None, None, "col"))
    return jax.shard_map(
        local,
        mesh=mesh,
        in_specs=placed,
        out_specs=(P("segment", None, "col"), P("segment", None)),
        check_vma=False,
    )
```

```python
import functools

import jax
import jax.numpy as jnp
from jax import lax
from jax.experimental import pallas as pl
from jax.experimental.pallas import tpu as pltpu
from jax.sharding import PartitionSpec as P

BATCHES = 3
RING = 4

epsilon = 1e-06

VMEM = pl.BlockSpec(memory_space=pltpu.VMEM)
SMEM = pl.BlockSpec(memory_space=pltpu.SMEM)
LIMIT = pltpu.CompilerParams(vmem_limit_bytes=24 * 1024 * 1024)


def chips_of(z, y, holder):
    sign = 1 - 2 * holder
    for step_y, step_z in ((0, 0), (0, sign), (1, 0), (-1, sign)):
        for step in range(2):
            from_y = (y - step_y - 2 * holder) & (RING - 1)
            from_z = (z - step_z - 2 * step) & (RING - 1)
            yield from_z * RING + from_y


def as_column(row, rows):
    lanes = row.shape[1]
    return jnp.broadcast_to(row, (8, lanes)).T[:rows, 0:1]


def as_row(column, lanes):
    rows = column.shape[0]
    if rows < lanes:
        column = jnp.concatenate([column, jnp.zeros((lanes - rows, 1), jnp.float32)], axis=0)
    return jnp.broadcast_to(column, (lanes, 128)).T[0:8]


def largest_lanes(rows):
    return -(-rows // 128) * 128


def hold_kernel(tensor_ref, after_ref, held_ref, arrived):
    copies = []
    pieces = arrived.shape[0]
    depth = tensor_ref.shape[1] // pieces
    for k in range(pieces):
        part = pl.ds(k * depth, depth)
        copy = pltpu.make_async_copy(tensor_ref.at[:, part, :], held_ref.at[:, part, :], arrived.at[k])
        copy.start()
        copies.append(copy)
    for copy in copies:
        copy.wait()


def hold(tensor, after):
    return pl.pallas_call(
        hold_kernel,
        out_shape=jax.ShapeDtypeStruct(tensor.shape, tensor.dtype),
        in_specs=[pl.BlockSpec(memory_space=pltpu.HBM), pl.BlockSpec(memory_space=pl.ANY)],
        out_specs=VMEM,
        scratch_shapes=[pltpu.SemaphoreType.DMA((4,))],
        compiler_params=LIMIT,
        name="hold",
    )(pltpu.with_memory_space_constraint(tensor, pltpu.HBM), after)


def site_kernel(tick, following, batches, place_ref, *refs):
    held_refs, refs = refs[:2 * RING], refs[2 * RING:]
    bit_ref, tensor_ref, refs = refs[0], refs[1], refs[2:]
    rows, width = held_refs[0].shape[1:]
    segment, z, y, core = (place_ref[i] for i in range(4))
    work = []
    for group in range(2):
        holder = core ^ group
        for k, chip in enumerate(chips_of(z, y, holder)):
            for side in range(2):
                start = pl.multiple_of((chip * 2 + (holder ^ side)) * width, width)
                work.append((held_refs[group * RING + k // 2], 2 * (k % 2) + side, start))
    totals = [jnp.zeros((rows, width), jnp.float32) for _ in range(2)]
    largest = jnp.zeros((rows, width), jnp.bfloat16)
    for ref, index, start in work:
        piece = ref[index]
        for bit in range(2):
            totals[bit] += jnp.dot(
                piece, tensor_ref[bit, pl.ds(start, width), :], preferred_element_type=jnp.float32
            )
        largest = jnp.maximum(largest, jnp.abs(piece))
    divisor = jnp.max(largest.astype(jnp.float32), axis=1, keepdims=True) + epsilon
    divisor = jnp.where(segment == 0, 1.0, divisor)
    position = jnp.clip(tick - segment, 0, batches - 1)
    bits = as_column(bit_ref[pl.ds(position, 1), :].astype(jnp.float32), rows)
    product = jnp.where(bits > 0.5, totals[1], totals[0]) * (1.0 / divisor)
    lanes = largest_lanes(rows)
    local = as_row(jnp.max(jnp.abs(product), axis=1, keepdims=True) + epsilon, lanes)
    if following is None:
        largest_refs, (product_ref, maxima_ref) = refs[:-2], refs[-2:]
        product_ref[...] = product
        everything = [ref[0:1, :] for ref in largest_refs] + [local[0:1]]
        for segment_here in range(RING):
            @pl.when(segment == segment_here)
            def _():
                taken = jnp.concatenate(everything[segment_here:segment_here + batches], axis=0)
                for i in range(maxima_ref.shape[0]):
                    maxima_ref[i] = taken
        return
    left_ref, product_ref, largest_ref, block_ref = refs
    product_ref[...] = product
    largest_ref[...] = local
    block_ref[...] = jnp.where(
        segment == RING - 1, left_ref[pl.ds(following * rows, rows), :], product.astype(jnp.bfloat16)
    )


def site(tick, following, place, held, bits, tensor, extra, cols):
    rows, width = held[0].shape[1:]
    batches = bits.shape[0]
    product = jax.ShapeDtypeStruct((rows, width), jnp.float32)
    if following is None:
        out_shape = (
            product,
            jax.ShapeDtypeStruct((cols, batches, largest_lanes(rows)), jnp.float32),
        )
    else:
        out_shape = (
            product,
            jax.ShapeDtypeStruct((8, largest_lanes(rows)), jnp.float32),
            jax.ShapeDtypeStruct((rows, width), jnp.bfloat16),
        )
    return pl.pallas_call(
        functools.partial(site_kernel, tick, following, batches),
        out_shape=out_shape,
        in_specs=[SMEM] + [VMEM] * (len(held) + 2 + len(extra)),
        out_specs=(VMEM,) * len(out_shape),
        compiler_params=LIMIT,
        name="site",
    )(place, *held, bits, tensor, *extra)


def finish_kernel(place_ref, maxima_ref, *refs):
    product_refs, (env_ref, log_ref) = refs[:-2], refs[-2:]
    rows, width = product_refs[0].shape
    maximum = jnp.max(maxima_ref[...], axis=0)
    logs = jnp.log(maximum)
    inverse = 1.0 / maximum
    for batch in range(maximum.shape[0]):
        log_ref[0:1, batch * rows:(batch + 1) * rows] = logs[batch:batch + 1, :rows]
        column = as_column(inverse[batch:batch + 1], rows)
        for segment in range(RING):
            @pl.when(place_ref[0] == segment)
            def _():
                product = product_refs[batch + segment][...]
                env_ref[0, batch * rows:(batch + 1) * rows, :] = (product * column).astype(jnp.bfloat16)


def finish(place, maxima, products):
    rows, width = products[0].shape
    batches = maxima.shape[1]
    return pl.pallas_call(
        finish_kernel,
        out_shape=(
            jax.ShapeDtypeStruct((1, batches * rows, width), jnp.bfloat16),
            jax.ShapeDtypeStruct((1, batches * rows), jnp.float32),
        ),
        in_specs=[SMEM] + [VMEM] * (1 + len(products)),
        out_specs=(VMEM, VMEM),
        compiler_params=LIMIT,
        name="finish",
    )(place, maxima, *products)


def moved(value, where):
    places = [
        (s, z, y, c)
        for s in range(RING) for z in range(RING) for y in range(RING) for c in range(2)
    ]
    number = {place: i for i, place in enumerate(places)}
    pairs = []
    for place in places:
        s, z, y, c = where(*place)
        pairs.append((number[place], number[(s % RING, z % RING, y % RING, c)]))
    return lax.ppermute(value, ("segment", "col"), pairs)


def swapped(value):
    return moved(value, lambda s, z, y, c: (s, z, y, 1 - c))


def gathered(block, other):
    both = jnp.stack([block, other])
    first = jnp.concatenate([
        moved(both, lambda s, z, y, c, d=d: (s + 1, z + 2 * d, y + 2 * c, c)) for d in range(2)
    ])
    return [
        first,
        moved(first, lambda s, z, y, c: (s, z + 1 - 2 * c, y, c)),
        moved(first, lambda s, z, y, c: (s, z, y + 1, c)),
        moved(first, lambda s, z, y, c: (s, z + 1 - 2 * c, y - 1, c)),
    ]


def local(left_env, bit_strings, site_tensors):
    cols = lax.axis_size("col")
    col = lax.axis_index("col")
    place = jnp.stack(
        [lax.axis_index("segment"), col // (2 * RING), (col // 2) % RING, col % 2]
    ).astype(jnp.int32)
    row_count, width = left_env.shape
    rows = row_count // BATCHES
    ticks = BATCHES + RING - 1
    bits = bit_strings.reshape(BATCHES, rows)
    tensor = None
    block, other = left_env[:rows], swapped(left_env)[:rows]
    products, largest = [], []
    for tick in range(ticks):
        held = gathered(block, swapped(block) if tick > 0 else other)
        if tensor is None:
            tensor = hold(site_tensors[0], held[0])
            held, tensor, bits, place = lax.optimization_barrier((held, tensor, bits, place))
        held += [swapped(piece) for piece in held]
        if tick + 1 < ticks:
            following = min(tick + 1, BATCHES - 1)
            product, most, block = site(tick, following, place, held, bits, tensor, [left_env], cols)
            largest.append(most)
        else:
            product, maxima = site(tick, None, place, held, bits, tensor, largest, cols)
        products.append(product)

    maxima = lax.all_to_all(maxima, "col", 0, 0, tiled=True)
    return finish(place, maxima, products)


def solution(mesh):
    placed = (P(None, "col"), P(None, "segment"), P("segment", None, None, "col"))
    return jax.shard_map(
        local,
        mesh=mesh,
        in_specs=placed,
        out_specs=(P("segment", None, "col"), P("segment", None)),
        check_vma=False,
    )
```

```python
import functools

import jax
import jax.numpy as jnp
from jax import lax
from jax.experimental import pallas as pl
from jax.experimental.pallas import tpu as pltpu
from jax.sharding import PartitionSpec as P

BATCHES = 3
RING = 4

epsilon = 1e-06

VMEM = pl.BlockSpec(memory_space=pltpu.VMEM)
SMEM = pl.BlockSpec(memory_space=pltpu.SMEM)
LIMIT = pltpu.CompilerParams(vmem_limit_bytes=24 * 1024 * 1024)


def chips_of(z, y, holder):
    sign = 1 - 2 * holder
    for step_y, step_z in ((0, 0), (0, sign), (1, 0), (-1, sign)):
        for step in range(2):
            from_y = (y - step_y - 2 * holder) & (RING - 1)
            from_z = (z - step_z - 2 * step) & (RING - 1)
            yield from_z * RING + from_y


def as_column(row, rows):
    lanes = row.shape[1]
    return jnp.broadcast_to(row, (8, lanes)).T[:rows, 0:1]


def as_row(column, lanes):
    rows = column.shape[0]
    if rows < lanes:
        column = jnp.concatenate([column, jnp.zeros((lanes - rows, 1), jnp.float32)], axis=0)
    return jnp.broadcast_to(column, (lanes, 128)).T[0:8]


def largest_lanes(rows):
    return -(-rows // 128) * 128


def hold_kernel(tensor_ref, after_ref, held_ref, arrived):
    copies = []
    pieces = arrived.shape[0]
    depth = tensor_ref.shape[1] // pieces
    for k in range(pieces):
        part = pl.ds(k * depth, depth)
        copy = pltpu.make_async_copy(tensor_ref.at[:, part, :], held_ref.at[:, part, :], arrived.at[k])
        copy.start()
        copies.append(copy)
    for copy in copies:
        copy.wait()


def hold(tensor, after):
    return pl.pallas_call(
        hold_kernel,
        out_shape=jax.ShapeDtypeStruct(tensor.shape, tensor.dtype),
        in_specs=[pl.BlockSpec(memory_space=pltpu.HBM), pl.BlockSpec(memory_space=pl.ANY)],
        out_specs=VMEM,
        scratch_shapes=[pltpu.SemaphoreType.DMA((4,))],
        compiler_params=LIMIT,
        name="hold",
    )(pltpu.with_memory_space_constraint(tensor, pltpu.HBM), after)


def site_kernel(tick, following, batches, place_ref, *refs):
    held_refs, refs = refs[:2 * RING], refs[2 * RING:]
    bit_ref, tensor_ref, refs = refs[0], refs[1], refs[2:]
    rows, width = held_refs[0].shape[1:]
    segment, z, y, core = (place_ref[i] for i in range(4))
    work = []
    for group in range(2):
        holder = core ^ group
        for k, chip in enumerate(chips_of(z, y, holder)):
            for side in range(2):
                start = pl.multiple_of((chip * 2 + (holder ^ side)) * width, width)
                work.append((held_refs[group * RING + k // 2], 2 * (k % 2) + side, start))
    totals = [jnp.zeros((rows, width), jnp.float32) for _ in range(2)]
    largest = jnp.zeros((rows, width), jnp.bfloat16)
    for ref, index, start in work:
        piece = ref[index]
        for bit in range(2):
            totals[bit] += jnp.dot(
                piece, tensor_ref[bit, pl.ds(start, width), :], preferred_element_type=jnp.float32
            )
        largest = jnp.maximum(largest, jnp.abs(piece))
    divisor = jnp.max(largest.astype(jnp.float32), axis=1, keepdims=True) + epsilon
    divisor = jnp.where(segment == 0, 1.0, divisor)
    position = jnp.clip(tick - segment, 0, batches - 1)
    bits = as_column(bit_ref[pl.ds(position, 1), :].astype(jnp.float32), rows)
    product = jnp.where(bits > 0.5, totals[1], totals[0]) * (1.0 / divisor)
    local = jnp.max(jnp.abs(product), axis=1, keepdims=True) + epsilon
    if following is None:
        largest_refs, (product_ref, maxima_ref) = refs[:-2], refs[-2:]
        product_ref[...] = product
        lanes = maxima_ref.shape[2]
        newest = as_row(local, lanes)[0:1]
        for segment_here in range(RING):
            @pl.when(segment == segment_here)
            def _():
                taken = [
                    as_row(ref[:, 0:1], lanes)[0:1]
                    for ref in largest_refs[segment_here:segment_here + batches]
                ]
                taken = jnp.concatenate((taken + [newest])[:batches], axis=0)
                for i in range(maxima_ref.shape[0]):
                    maxima_ref[i] = taken
        return
    left_ref, product_ref, largest_ref, block_ref = refs
    product_ref[...] = product
    largest_ref[...] = jnp.broadcast_to(local, largest_ref.shape)
    block_ref[...] = jnp.where(
        segment == RING - 1, left_ref[pl.ds(following * rows, rows), :], product.astype(jnp.bfloat16)
    )


def site(tick, following, place, held, bits, tensor, extra, cols):
    rows, width = held[0].shape[1:]
    batches = bits.shape[0]
    product = jax.ShapeDtypeStruct((rows, width), jnp.float32)
    if following is None:
        out_shape = (
            product,
            jax.ShapeDtypeStruct((cols, batches, largest_lanes(rows)), jnp.float32),
        )
    else:
        out_shape = (
            product,
            jax.ShapeDtypeStruct((rows, 128), jnp.float32),
            jax.ShapeDtypeStruct((rows, width), jnp.bfloat16),
        )
    return pl.pallas_call(
        functools.partial(site_kernel, tick, following, batches),
        out_shape=out_shape,
        in_specs=[SMEM] + [VMEM] * (len(held) + 2 + len(extra)),
        out_specs=(VMEM,) * len(out_shape),
        compiler_params=LIMIT,
        name="site",
    )(place, *held, bits, tensor, *extra)


def finish_kernel(place_ref, maxima_ref, *refs):
    product_refs, (env_ref, log_ref) = refs[:-2], refs[-2:]
    rows, width = product_refs[0].shape
    maximum = jnp.max(maxima_ref[...], axis=0)
    logs = jnp.log(maximum)
    inverse = 1.0 / maximum
    for batch in range(maximum.shape[0]):
        log_ref[0:1, batch * rows:(batch + 1) * rows] = logs[batch:batch + 1, :rows]
        column = as_column(inverse[batch:batch + 1], rows)
        for segment in range(RING):
            @pl.when(place_ref[0] == segment)
            def _():
                product = product_refs[batch + segment][...]
                env_ref[0, batch * rows:(batch + 1) * rows, :] = (product * column).astype(jnp.bfloat16)


def finish(place, maxima, products):
    rows, width = products[0].shape
    batches = maxima.shape[1]
    return pl.pallas_call(
        finish_kernel,
        out_shape=(
            jax.ShapeDtypeStruct((1, batches * rows, width), jnp.bfloat16),
            jax.ShapeDtypeStruct((1, batches * rows), jnp.float32),
        ),
        in_specs=[SMEM] + [VMEM] * (1 + len(products)),
        out_specs=(VMEM, VMEM),
        compiler_params=LIMIT,
        name="finish",
    )(place, maxima, *products)


def moved(value, where):
    places = [
        (s, z, y, c)
        for s in range(RING) for z in range(RING) for y in range(RING) for c in range(2)
    ]
    number = {place: i for i, place in enumerate(places)}
    pairs = []
    for place in places:
        s, z, y, c = where(*place)
        pairs.append((number[place], number[(s % RING, z % RING, y % RING, c)]))
    return lax.ppermute(value, ("segment", "col"), pairs)


def swapped(value):
    return moved(value, lambda s, z, y, c: (s, z, y, 1 - c))


def gathered(block, other):
    both = jnp.stack([block, other])
    first = jnp.concatenate([
        moved(both, lambda s, z, y, c, d=d: (s + 1, z + 2 * d, y + 2 * c, c)) for d in range(2)
    ])
    early = swapped(first)
    first, early = lax.optimization_barrier((first, early))
    return [
        first,
        moved(first, lambda s, z, y, c: (s, z + 1 - 2 * c, y, c)),
        moved(first, lambda s, z, y, c: (s, z, y + 1, c)),
        moved(first, lambda s, z, y, c: (s, z + 1 - 2 * c, y - 1, c)),
    ]


def local(left_env, bit_strings, site_tensors):
    cols = lax.axis_size("col")
    col = lax.axis_index("col")
    place = jnp.stack(
        [lax.axis_index("segment"), col // (2 * RING), (col // 2) % RING, col % 2]
    ).astype(jnp.int32)
    row_count, width = left_env.shape
    rows = row_count // BATCHES
    ticks = BATCHES + RING - 1
    bits = bit_strings.reshape(BATCHES, rows)
    tensor = None
    block, other = left_env[:rows], swapped(left_env)[:rows]
    products, largest = [], []
    for tick in range(ticks):
        held = gathered(block, swapped(block) if tick > 0 else other)
        if tensor is None:
            tensor = hold(site_tensors[0], held[0])
            held[2], tensor, bits, place = lax.optimization_barrier((held[2], tensor, bits, place))
        held += [swapped(piece) for piece in held]
        if tick + 1 < ticks:
            following = min(tick + 1, BATCHES - 1)
            product, most, block = site(tick, following, place, held, bits, tensor, [left_env], cols)
            largest.append(most)
        else:
            product, maxima = site(tick, None, place, held, bits, tensor, largest, cols)
        products.append(product)

    maxima = lax.all_to_all(maxima, "col", 0, 0, tiled=True)
    return finish(place, maxima, products)


def solution(mesh):
    placed = (P(None, "col"), P(None, "segment"), P("segment", None, None, "col"))
    return jax.shard_map(
        local,
        mesh=mesh,
        in_specs=placed,
        out_specs=(P("segment", None, "col"), P("segment", None)),
        check_vma=False,
    )
```
